32 devices in a mesh: seq: 16 (over z, y, core), head: 2 (over x).
Axes of the slice: x: 2, y: 2, z: 4, core: 2. Of those that a mesh axis runs over, the one named last changes fastest.
Arguments:
- queries: bfloat16 [4096, 512], P('seq', 'head'), may hold values from -4 to 4
- values: bfloat16 [4096, 512], P('seq', 'head'), may hold values from -6 to 6
- scales: float32 [4096, 8], P('seq', 'head'), may hold values from 2 to 20
- block_reach: int32 [16], P('seq'), may hold values from 1 to 4
- out_weight: bfloat16 [512, 1024], P('head'), may hold values from -0.25 to 0.25
- out_grad: bfloat16 [4096, 512], P('seq', 'head'), may hold values from -6 to 6
Outputs:
- mixed: bfloat16 [4096, 1024], P(('seq', 'head'))
- value_grad: bfloat16 [4096, 512], P('seq', 'head')
The draws below stay inside these ranges and needn't reach their ends.
All inputs are finite; a program needn't handle non-finite values.
Results may differ from the reference program's by a relative error of at most 0.0015.
The reference program's roundings to bfloat16 on the way count: a program that leaves them out, or rounds other values in their place, can miss the bound.
Values may be sent and summed in bfloat16 or wider, within the bound.
No kernel may reach another device: no remote copies, remote signals or barrier semaphores. Data moves between devices by JAX's collectives and lax.ppermute only.
A program may use at most 64 MiB of HBM per device.

```python
import math
import jax
import jax.numpy as jnp
from jax import lax

D = 1024
HD = 64
WINDOW = 4
TOK_DEV = 256
HEADS = 8
NBLK = 16
TOKENS = 4096


def query_field(key):
    base_key = jax.random.fold_in(key, 11)
    scale_key = jax.random.fold_in(key, 12)
    logs = jax.random.uniform(scale_key, (TOKENS, HEADS), jnp.float32, math.log(2.0), math.log(20.0))
    spread = jnp.exp(logs)
    raw = jax.random.normal(base_key, (TOKENS, HEADS, HD), jnp.float32)
    return (jnp.clip(raw, -4.0, 4.0), jnp.clip(spread, 2.0, 20.0))


def draw_queries(key, part):
    field = query_field(key)[0]
    return field.reshape(TOKENS, HEADS * HD).astype(jnp.bfloat16)


def draw_scales(key, part):
    return query_field(key)[1]


def plant(values, own_key, smallest, high):
    place = [jax.random.randint(jax.random.fold_in(own_key, axis), (), 0, length) for axis, length in enumerate(values.shape)]
    main_axis = values.shape.index(max(values.shape))
    next_to = place[:main_axis] + [(place[main_axis] + 1) % values.shape[main_axis]] + place[main_axis + 1:]
    return values.at[tuple(place)].set(smallest).at[tuple(next_to)].set(high)


def level_of(stream_key, extent, pieces, least, top_value):
    gain, own = 1.0, jax.random.fold_in(stream_key, 6)
    for axis_at, shards_of in pieces:
        draws = jnp.exp(jax.random.uniform(jax.random.fold_in(own, axis_at), (shards_of,), jnp.float32, least / len(pieces), top_value / len(pieces)))
        gain = gain * jnp.repeat(draws, extent[axis_at] // shards_of).reshape([-1 if axis == axis_at else 1 for axis in range(len(extent))])
    return gain


def noise(own_key, dims, scale, most, pieces=(), held_as=jnp.bfloat16):
    loudness = level_of(own_key, dims, pieces, -0.22, 0.18) if pieces else 1.0
    entries = jax.random.normal(own_key, dims, jnp.float32) * scale * loudness
    return jnp.minimum(jnp.maximum(entries, -most), most).astype(held_as)


def setup_inputs(seed: int = 0) -> dict:
    key_of = jax.random.split(jax.random.key(seed), 7)
    queries = draw_queries(jax.random.fold_in(key_of[6], 71), 0)
    values = noise(key_of[1], (TOKENS, HEADS * HD), 1.0, 6.0, ((0, 16), (1, 2)))
    scales = draw_scales(jax.random.fold_in(key_of[6], 71), 0)
    block_reach = plant(jax.random.randint(key_of[3], (NBLK,), 1, WINDOW + 1), jax.random.fold_in(key_of[3], 1), 1, WINDOW).astype(jnp.int32)
    out_weight = noise(key_of[4], (HEADS * HD, D), (HEADS * HD) ** -0.5, 0.25, ((0, 2),))
    out_grad = noise(key_of[5], (TOKENS, HEADS * HD), 1.0, 6.0, ((0, 16), (1, 2)))
    return dict(queries=queries, values=values, scales=scales, block_reach=block_reach, out_weight=out_weight, out_grad=out_grad)


NEGATIVE = -1e+30

def rounded(tensor):
    return lax.optimization_barrier(tensor.astype(jnp.bfloat16)).astype(jnp.float32)

def unit_keys(queries, scales):
    as_float = queries.astype(jnp.float32).reshape(queries.shape[0], scales.shape[1], HD)
    direction = as_float * lax.rsqrt(lax.optimization_barrier(jnp.sum(as_float * as_float, axis=-1, keepdims=True)) + 1e-06)
    return (direction * scales[:, :, None]).astype(jnp.bfloat16)

def reference(queries, values, scales, block_reach, out_weight, out_grad):
    span = 2 * WINDOW + 1
    key_blocks = rounded(unit_keys(queries, scales)).reshape(NBLK, TOK_DEV, HEADS, HD)
    value_blocks = values.astype(jnp.float32).reshape(NBLK, TOK_DEV, HEADS, HD)
    grad_blocks = out_grad.astype(jnp.float32).reshape(NBLK, TOK_DEV, HEADS, HD)
    padding = jnp.zeros((WINDOW, TOK_DEV, HEADS, HD), jnp.float32)
    padded_keys = jnp.concatenate([padding, key_blocks, padding], axis=0)
    padded_values = jnp.concatenate([padding, value_blocks, padding], axis=0)
    padded_grads = jnp.concatenate([padding, grad_blocks, padding], axis=0)
    reach_pad = jnp.zeros((WINDOW,), jnp.int32)
    padded_reach = jnp.concatenate([reach_pad, block_reach.astype(jnp.int32), reach_pad], axis=0)
    offsets = jnp.arange(span, dtype=jnp.int32) - WINDOW
    diagonal = jnp.eye(TOK_DEV, dtype=bool)
    self_mask = (offsets == 0)[:, None, None, None] & diagonal[None, None, :, :]

    def allowed_near(block):
        nearby = lax.dynamic_slice_in_dim(padded_reach, block, span)
        limit = jnp.minimum(block_reach[block].astype(jnp.int32), nearby)
        return ((offsets == 0) | (jnp.abs(offsets) <= limit)).astype(jnp.float32)

    def forward_block(block):
        own_keys = key_blocks[block]
        near_keys = lax.dynamic_slice_in_dim(padded_keys, block, span, 0)
        near_values = lax.dynamic_slice_in_dim(padded_values, block, span, 0)
        scores = jnp.einsum('ihd,cjhd->chij', own_keys, near_keys)
        scores = jnp.where(self_mask, NEGATIVE, scores)
        allowed = allowed_near(block)[:, None, None]
        tile_top = lax.optimization_barrier(jnp.max(scores, axis=-1))
        exponent = jnp.exp(scores - tile_top[..., None]) * allowed[..., None]
        tile_sums = lax.optimization_barrier(jnp.sum(exponent, axis=-1))
        numerators = jnp.einsum('chij,cjhd->cihd', rounded(exponent), near_values)
        tile_top = jnp.where(allowed > 0, tile_top, NEGATIVE)
        row_top = lax.optimization_barrier(jnp.max(tile_top, axis=0))
        factors = jnp.exp(tile_top - row_top[None])
        totals = lax.optimization_barrier(jnp.sum(factors * tile_sums, axis=0))
        combined = lax.optimization_barrier(jnp.sum(jnp.transpose(factors, (0, 2, 1))[..., None] * numerators, axis=0))
        attended = (combined / jnp.transpose(totals)[:, :, None]).astype(jnp.bfloat16)
        return (attended, row_top, totals)
    attended, row_top, totals = lax.map(forward_block, jnp.arange(NBLK, dtype=jnp.int32))
    flat = attended.reshape(TOKENS, HEADS * HD)
    mixed = jnp.dot(flat, out_weight, preferred_element_type=jnp.float32).astype(jnp.bfloat16)
    padded_top = jnp.concatenate([jnp.zeros((WINDOW, HEADS, TOK_DEV), jnp.float32), row_top, jnp.zeros((WINDOW, HEADS, TOK_DEV), jnp.float32)], axis=0)
    padded_total = jnp.concatenate([jnp.ones((WINDOW, HEADS, TOK_DEV), jnp.float32), totals, jnp.ones((WINDOW, HEADS, TOK_DEV), jnp.float32)], axis=0)

    def grad_block(block):
        own_keys = key_blocks[block]
        near_keys = lax.dynamic_slice_in_dim(padded_keys, block, span, 0)
        near_grads = lax.dynamic_slice_in_dim(padded_grads, block, span, 0)
        near_top = lax.dynamic_slice_in_dim(padded_top, block, span, 0)
        near_total = lax.dynamic_slice_in_dim(padded_total, block, span, 0)
        scores = jnp.einsum('bihd,jhd->bhij', near_keys, own_keys)
        scores = jnp.where(self_mask, NEGATIVE, scores)
        allowed = allowed_near(block)[:, None, None, None]
        weights = jnp.where(allowed > 0, jnp.exp(scores - near_top[..., None]) / near_total[..., None], 0.0)
        return jnp.einsum('bhij,bihd->jhd', rounded(weights), near_grads).astype(jnp.bfloat16)
    value_grad = lax.map(grad_block, jnp.arange(NBLK, dtype=jnp.int32)).reshape(TOKENS, HEADS * HD)
    return (mixed, value_grad)
```

```python
import jax
import jax.numpy as jnp
from jax import lax
from jax.experimental import pallas as pl
from jax.experimental.pallas import tpu as pltpu
from jax.sharding import PartitionSpec as P

HD = 64
NEGATIVE = -1e30
REACH_ROWS = 16
F32 = jnp.float32
BF16 = jnp.bfloat16


def sibling(value):
    count = lax.axis_size("seq")
    return lax.ppermute(value, "seq", [(i, i ^ 1) for i in range(count)])


def chip_ring(value, step):
    chips = lax.axis_size("seq") // 2
    pairs = []
    for chip in range(chips):
        up, down = chip + step, chip - step
        pairs.append((2 * chip, 2 * up if up < chips else 2 * chip + 1))
        pairs.append((2 * chip + 1, 2 * down + 1 if down >= 0 else 2 * chip))
    return lax.ppermute(value, "seq", pairs)


def other_head(value):
    return lax.ppermute(value, "head", [(0, 1), (1, 0)])


def dot_nt(a, b):
    return lax.dot_general(a, b, (((1,), (1,)), ((), ())), preferred_element_type=F32)


def dot_nn(a, b):
    return lax.dot_general(a, b, (((1,), (0,)), ((), ())), preferred_element_type=F32)


def prepare_body(reach_ref, q_ref, s_ref, v_ref, k_ref, vt_ref):
    length, width = q_ref.shape
    low = lax.broadcasted_iota(jnp.int32, (length, 128), 1) < HD
    for g in range(width // 128):
        lanes = slice(128 * g, 128 * g + 128)
        q = q_ref[:, lanes].astype(F32)
        square = q * q
        sum_low = jnp.sum(jnp.where(low, square, 0.0), axis=1, keepdims=True)
        sum_high = jnp.sum(jnp.where(low, 0.0, square), axis=1, keepdims=True)
        inverse = jnp.where(low, lax.rsqrt(sum_low + 1e-6), lax.rsqrt(sum_high + 1e-6))
        scale = jnp.where(low, s_ref[:, 2 * g : 2 * g + 1], s_ref[:, 2 * g + 1 : 2 * g + 2])
        k_ref[0:length, lanes] = ((q * inverse) * scale).astype(BF16)
    reach = jnp.full((REACH_ROWS, width), reach_ref[0].astype(F32), F32)
    k_ref[length:, :] = reach.astype(BF16)
    vt_ref[...] = jnp.transpose(v_ref[...].astype(F32)).astype(BF16)


def head_keys(k_ref, length, h):
    g = h // 2
    lane = lax.broadcasted_iota(jnp.int32, (length, 128), 1)
    keep = (lane < HD) if h % 2 == 0 else (lane >= HD)
    rows = k_ref[0:length, 128 * g : 128 * g + 128]
    return jnp.where(keep, rows, jnp.zeros_like(rows))


def far_slots(flag_ref, length, sib, one, two, one_s, two_s):
    return [
        (sib, 0, 1, None),
        (one, 0, 2, flag_ref[1]),
        (one, 1, 1, flag_ref[1]),
        (two, 0, 4, flag_ref[2]),
        (two, 1, 3, flag_ref[2]),
        (one_s, 0, 3, flag_ref[3]),
        (one_s, 1, 2, flag_ref[3]),
        (two_s, 1, 4, flag_ref[4]),
    ]


def slot_allowed(flag_ref, slot, length):
    ref, block, distance, valid = slot
    start = block * (length + REACH_ROWS) + length
    far = jnp.max(ref[start : start + REACH_ROWS, 0:128].astype(F32))
    near = flag_ref[0].astype(F32)
    allowed = jnp.minimum(near, far) >= float(distance)
    if valid is not None:
        allowed = jnp.logical_and(allowed, valid > 0)
    return allowed


def diagonal(length):
    row = lax.broadcasted_iota(jnp.int32, (length, length), 0)
    return row == lax.broadcasted_iota(jnp.int32, (length, length), 1)


def stats_body(flag_ref, own, sib, one, two, one_s, two_s, st_ref, m_ref):
    length = own.shape[0] - REACH_ROWS
    heads = own.shape[1] // HD
    keys = [head_keys(own, length, h) for h in range(heads)]

    def tile(slot, ref, row, masked):
        for h in range(heads):
            g = h // 2
            scores = dot_nt(ref[row : row + length, 128 * g : 128 * g + 128], keys[h])
            if masked:
                scores = jnp.where(diagonal(length), NEGATIVE, scores)
            top = jnp.max(scores, axis=0, keepdims=True)
            total = jnp.sum(jnp.exp(scores - top), axis=0, keepdims=True)
            m_ref[2 * heads * slot + h : 2 * heads * slot + h + 1, :] = top
            m_ref[2 * heads * slot + heads + h : 2 * heads * slot + heads + h + 1, :] = total

    tile(0, own, 0, True)
    slots = far_slots(flag_ref, length, sib, one, two, one_s, two_s)
    for index, slot in enumerate(slots):
        at = index + 1
        m_ref[2 * heads * at : 2 * heads * at + heads, :] = jnp.full((heads, length), NEGATIVE, F32)
        m_ref[2 * heads * at + heads : 2 * heads * at + 2 * heads, :] = jnp.zeros((heads, length), F32)

        @pl.when(slot_allowed(flag_ref, slot, length))
        def _():
            tile(at, slot[0], slot[1] * (length + REACH_ROWS), False)

    tops = [m_ref[2 * heads * s : 2 * heads * s + heads, :] for s in range(len(slots) + 1)]
    top = tops[0]
    for other in tops[1:]:
        top = jnp.maximum(top, other)
    total = jnp.zeros((heads, length), F32)
    for s in range(len(slots) + 1):
        total = total + jnp.exp(tops[s] - top) * m_ref[2 * heads * s + heads : 2 * heads * s + 2 * heads, :]
    st_ref[0:heads, :] = top
    st_ref[heads : 2 * heads, :] = total


def attend_body(
    flag_ref, own, sib, one, two, one_s, two_s, v, vsib, vone, vtwo, vone_s, vtwo_s,
    st_ref, m_ref, keep_ref, send_ref, acc, rows_ref,
):
    length = own.shape[0] - REACH_ROWS
    heads = own.shape[1] // HD
    keys = [head_keys(own, length, h) for h in range(heads)]

    def tile(slot, ref, row, vref, vrow, masked):
        for h in range(heads):
            g = h // 2
            scores = dot_nt(ref[row : row + length, 128 * g : 128 * g + 128], keys[h])
            if masked:
                scores = jnp.where(diagonal(length), NEGATIVE, scores)
            top = m_ref[2 * heads * slot + h : 2 * heads * slot + h + 1, :]
            weights = jnp.exp(scores - top).astype(BF16)
            numer = dot_nn(vref[vrow + HD * h : vrow + HD * h + HD, :], weights)
            numer = numer * jnp.exp(top - st_ref[h : h + 1, :])
            if masked:
                acc[HD * h : HD * h + HD, :] = numer
            else:
                acc[HD * h : HD * h + HD, :] += numer

    tile(0, own, 0, v, 0, True)
    vrefs = [vsib, vone, vone, vtwo, vtwo, vone_s, vone_s, vtwo_s]
    slots = far_slots(flag_ref, length, sib, one, two, one_s, two_s)
    for index, slot in enumerate(slots):

        @pl.when(slot_allowed(flag_ref, slot, length))
        def _():
            row = slot[1] * (length + REACH_ROWS)
            tile(index + 1, slot[0], row, vrefs[index], slot[1] * heads * HD, False)

    for h in range(heads):
        part = slice(HD * h, HD * h + HD)
        acc[part, :] = acc[part, :] / st_ref[heads + h : heads + h + 1, :]
    rows_ref[...] = jnp.transpose(acc[...])
    half = length // 2
    mine = flag_ref[5]
    keep_ref[...] = rows_ref[pl.ds(pl.multiple_of(mine * half, half), half), :].astype(BF16)
    send_ref[...] = rows_ref[pl.ds(pl.multiple_of((1 - mine) * half, half), half), :].astype(BF16)


def grad_body(
    flag_ref, own, sib, one, two, one_s, two_s, g0, gsib, gone, gtwo, gone_s, gtwo_s,
    st, ssib, sone, stwo, sone_s, stwo_s, out_ref, acc,
):
    length = own.shape[0] - REACH_ROWS
    heads = own.shape[1] // HD
    keys = [head_keys(own, length, h) for h in range(heads)]
    low = lax.broadcasted_iota(jnp.int32, (length, 128), 1) < HD

    def tile(ref, row, gref, grow, sref, srow, masked):
        for g in range(heads // 2):
            lanes = slice(128 * g, 128 * g + 128)
            grads = gref[grow : grow + length, lanes]
            parts = []
            for h in (2 * g, 2 * g + 1):
                scores = dot_nt(keys[h], ref[row : row + length, lanes])
                if masked:
                    scores = jnp.where(diagonal(length), NEGATIVE, scores)
                top = sref[srow + h : srow + h + 1, :]
                inverse = 1.0 / sref[srow + heads + h : srow + heads + h + 1, :]
                weights = (jnp.exp(scores - top) * inverse).astype(BF16)
                zero = jnp.zeros_like(grads)
                some = jnp.where(low, grads, zero) if h % 2 == 0 else jnp.where(low, zero, grads)
                parts.append(dot_nn(weights, some))
            if masked:
                acc[:, lanes] = parts[0] + parts[1]
            else:
                acc[:, lanes] += parts[0] + parts[1]

    tile(own, 0, g0, 0, st, 0, True)
    grefs = [gsib, gone, gone, gtwo, gtwo, gone_s, gone_s, gtwo_s]
    srefs = [ssib, sone, sone, stwo, stwo, sone_s, sone_s, stwo_s]
    slots = far_slots(flag_ref, length, sib, one, two, one_s, two_s)
    for index, slot in enumerate(slots):

        @pl.when(slot_allowed(flag_ref, slot, length))
        def _():
            block = slot[1]
            row = block * (length + REACH_ROWS)
            tile(slot[0], row, grefs[index], block * length, srefs[index], 2 * heads * block, False)

    out_ref[...] = acc[...].astype(BF16)


def project_body(keep_ref, got_ref, near_ref, far_ref, out_ref):
    total = dot_nn(keep_ref[...], near_ref[...]) + dot_nn(got_ref[...], far_ref[...])
    out_ref[...] = total.astype(BF16)


VMEM = pl.BlockSpec(memory_space=pltpu.VMEM)
SMEM = pl.BlockSpec(memory_space=pltpu.SMEM)


def call(body, name, args, outs, smem=1, scratch=()):
    specs = [SMEM] * smem + [VMEM] * (len(args) - smem)
    return pl.pallas_call(
        body,
        name=name,
        in_specs=specs,
        out_specs=[VMEM] * len(outs),
        out_shape=[jax.ShapeDtypeStruct(shape, dtype) for shape, dtype in outs],
        scratch_shapes=[pltpu.VMEM(shape, dtype) for shape, dtype in scratch],
    )(*args)


def gathered(own):
    sib = sibling(own)
    both = jnp.concatenate([own, sib], axis=0)
    one, two = chip_ring(both, 1), chip_ring(both, 2)
    return [own, sib, one, two, sibling(one), sibling(two)]


def shards(queries, values, scales, block_reach, out_weight, out_grad):
    length, width = queries.shape
    heads = scales.shape[1]
    chips = lax.axis_size("seq") // 2
    place = lax.axis_index("seq")
    chip, toward = place // 2, 2 * (place % 2) - 1
    inside = lambda c: jnp.logical_and(c >= 0, c < chips).astype(jnp.int32)
    flags = jnp.stack(
        [
            block_reach[0],
            inside(chip + toward),
            inside(chip + 2 * toward),
            inside(chip - toward),
            inside(chip - 2 * toward),
            lax.axis_index("head"),
        ]
    ).astype(jnp.int32)
    keys, turned = call(
        prepare_body,
        "prepare",
        [block_reach, queries, scales, values],
        [((length + REACH_ROWS, width), BF16), ((width, length), BF16)],
    )
    key_set = gathered(keys)
    value_set = gathered(turned)
    grad_set = gathered(out_grad)
    far_weight = other_head(out_weight)
    stats, tops = call(
        stats_body,
        "stats",
        [flags, *key_set],
        [((2 * heads, length), F32), ((9 * 2 * heads, length), F32)],
    )
    stat_set = gathered(stats)
    keep, send = call(
        attend_body,
        "attend",
        [flags, *key_set, *value_set, stats, tops],
        [((length // 2, width), BF16), ((length // 2, width), BF16)],
        scratch=[((width, length), F32), ((length, width), F32)],
    )
    got = other_head(send)
    (value_grad,) = call(
        grad_body,
        "value_grad",
        [flags, *key_set, *grad_set, *stat_set],
        [((length, width), BF16)],
        scratch=[((length, width), F32)],
    )
    (mixed,) = call(
        project_body,
        "project",
        [keep, got, out_weight, far_weight],
        [((length // 2, out_weight.shape[1]), BF16)],
        smem=0,
    )
    return (mixed, value_grad)


def solution(mesh):
    return jax.shard_map(
        shards,
        mesh=mesh,
        in_specs=(
            P("seq", "head"),
            P("seq", "head"),
            P("seq", "head"),
            P("seq"),
            P("head", None),
            P("seq", "head"),
        ),
        out_specs=(P(("seq", "head"), None), P("seq", "head")),
        check_vma=False,
    )
```

```python
from functools import partial

import jax
import jax.numpy as jnp
from jax import lax
from jax.experimental import pallas as pl
from jax.experimental.pallas import tpu as pltpu
from jax.sharding import PartitionSpec as P


HD = 64
NEGATIVE = -1e30
REACH_ROWS = 16
F32 = jnp.float32
BF16 = jnp.bfloat16


def sibling(value):
    count = lax.axis_size("seq")
    return lax.ppermute(value, "seq", [(i, i ^ 1) for i in range(count)])


def chip_ring(value, step):
    chips = lax.axis_size("seq") // 2
    pairs = []
    for chip in range(chips):
        up, down = chip + step, chip - step
        pairs.append((2 * chip, 2 * up if up < chips else 2 * chip + 1))
        pairs.append((2 * chip + 1, 2 * down + 1 if down >= 0 else 2 * chip))
    return lax.ppermute(value, "seq", pairs)


def other_head(value):
    return lax.ppermute(value, "head", [(0, 1), (1, 0)])


def dot_nt(a, b):
    return lax.dot_general(a, b, (((1,), (1,)), ((), ())), preferred_element_type=F32)


def dot_nn(a, b):
    return lax.dot_general(a, b, (((1,), (0,)), ((), ())), preferred_element_type=F32)


def prepare_body(
    reach_ref, q_in, s_in, v_in, g_in, k_ref, vt_ref, g_ref, q_ref, s_ref, v_ref, sems
):
    length, width = q_ref.shape
    pairs = ((q_in, q_ref), (s_in, s_ref), (v_in, v_ref), (g_in, g_ref))
    copies = [pltpu.make_async_copy(a, b, sems.at[i]) for i, (a, b) in enumerate(pairs)]
    for copy in copies:
        copy.start()
    copies[0].wait()
    copies[1].wait()
    low = lax.broadcasted_iota(jnp.int32, (length, 128), 1) < HD
    scales = jnp.transpose(s_ref[...])
    for g in range(width // 128):
        lanes = slice(128 * g, 128 * g + 128)
        q = q_ref[:, lanes].astype(F32)
        square = q * q
        sum_low = jnp.sum(jnp.where(low, square, 0.0), axis=1, keepdims=True)
        sum_high = jnp.sum(jnp.where(low, 0.0, square), axis=1, keepdims=True)
        inverse = jnp.where(low, lax.rsqrt(sum_low + 1e-6), lax.rsqrt(sum_high + 1e-6))
        scale = jnp.where(low, scales[:, 2 * g : 2 * g + 1], scales[:, 2 * g + 1 : 2 * g + 2])
        k_ref[0:length, lanes] = ((q * inverse) * scale).astype(BF16)
    reach = jnp.full((REACH_ROWS, width), reach_ref[0].astype(F32), F32)
    k_ref[length:, :] = reach.astype(BF16)
    copies[2].wait()
    vt_ref[...] = jnp.transpose(v_ref[...].astype(F32)).astype(BF16)
    copies[3].wait()


def head_keys(k_ref, length, h):
    g = h // 2
    lane = lax.broadcasted_iota(jnp.int32, (length, 128), 1)
    keep = (lane < HD) if h % 2 == 0 else (lane >= HD)
    rows = k_ref[0:length, 128 * g : 128 * g + 128]
    return jnp.where(keep, rows, jnp.zeros_like(rows))


def far_slots(chips, sib, one, two, one_s, two_s):
    place = lax.axis_index("seq")
    odd = lax.rem(place, 2)
    chip, toward = lax.div(place, 2), 2 * odd - 1

    def inside(step):
        far = chip + step * toward
        return jnp.logical_and(far >= 0, far < chips)

    return [
        (sib, 0, 1, None),
        (one, 0, 2, inside(1)),
        (one, 1, 1, inside(1)),
        (two, 0, 4, inside(2)),
        (two, 1, 3, inside(2)),
        (one_s, 0, 3, inside(-1)),
        (one_s, 1, 2, inside(-1)),
        (two_s, 1, 4, inside(-2)),
    ]


def allowed_slots(reach_ref, slots, length):
    near = reach_ref[0].astype(F32)
    result = []
    for ref, block, distance, valid in slots:
        start = block * (length + REACH_ROWS) + length
        far = jnp.max(ref[start : start + REACH_ROWS, 0:128].astype(F32))
        allowed = jnp.minimum(near, far) >= float(distance)
        if valid is not None:
            allowed = jnp.logical_and(allowed, valid)
        result.append(allowed)
    return result


def off_diagonal(scores, row, column):
    rows = lax.broadcasted_iota(jnp.int32, scores.shape, 0) + row
    columns = lax.broadcasted_iota(jnp.int32, scores.shape, 1) + column
    return jnp.where(rows == columns, NEGATIVE, scores)


def stats_body(chips, reach_ref, own, sib, one, two, one_s, two_s, st_ref, m_ref, w_ref):
    length = own.shape[0] - REACH_ROWS
    heads = own.shape[1] // HD
    keys = [head_keys(own, length, h) for h in range(heads)]

    def tile(slot, ref, row, masked):
        for h in range(heads):
            g = h // 2
            rows = ref[row : row + length, 128 * g : 128 * g + 128]
            for part in range(0, length, 128):
                scores = dot_nt(rows, keys[h][part : part + 128, :])
                if masked:
                    scores = off_diagonal(scores, 0, part)
                top = jnp.max(scores, axis=0, keepdims=True)
                exponent = jnp.exp(scores - top)
                total = jnp.sum(exponent, axis=0, keepdims=True)
                lanes = slice(part, part + 128)
                at = 2 * heads * slot + h
                m_ref[at : at + 1, lanes] = top
                m_ref[at + heads : at + heads + 1, lanes] = total
                at = (slot * heads + h) * length
                w_ref[at : at + length, lanes] = exponent.astype(BF16)

    slots = far_slots(chips, sib, one, two, one_s, two_s)
    allowed = allowed_slots(reach_ref, slots, length)
    tile(0, own, 0, True)
    for index, slot in enumerate(slots):
        at = 2 * heads * (index + 1)
        m_ref[at : at + heads, :] = jnp.full((heads, length), NEGATIVE, F32)
        m_ref[at + heads : at + 2 * heads, :] = jnp.zeros((heads, length), F32)

        @pl.when(allowed[index])
        def _():
            tile(index + 1, slot[0], slot[1] * (length + REACH_ROWS), False)

    count = len(slots) + 1
    tops = [m_ref[2 * heads * s : 2 * heads * s + heads, :] for s in range(count)]
    top = tops[0]
    for other in tops[1:]:
        top = jnp.maximum(top, other)
    total = jnp.zeros((heads, length), F32)
    for s in range(count):
        at = 2 * heads * s
        factor = jnp.exp(tops[s] - top)
        total = total + factor * m_ref[at + heads : at + 2 * heads, :]
        m_ref[at : at + heads, :] = factor
    st_ref[0:heads, :] = top + jnp.log(total)
    st_ref[heads : 2 * heads, :] = total


def attend_body(
    chips, reach_ref, own, sib, one, two, one_s, two_s, v, vsib, vone, vtwo, vone_s, vtwo_s,
    st_ref, m_ref, w_ref, keep_ref, send_ref, acc, rows_ref,
):
    length = own.shape[0] - REACH_ROWS
    heads = own.shape[1] // HD

    def tile(slot, vref, vrow):
        for h in range(heads):
            at = (slot * heads + h) * length
            part = slice(HD * h, HD * h + HD)
            numer = dot_nn(vref[vrow + HD * h : vrow + HD * h + HD, :], w_ref[at : at + length, :])
            numer = numer * m_ref[2 * heads * slot + h : 2 * heads * slot + h + 1, :]
            if slot == 0:
                acc[part, :] = numer
            else:
                acc[part, :] += numer

    slots = far_slots(chips, sib, one, two, one_s, two_s)
    allowed = allowed_slots(reach_ref, slots, length)
    tile(0, v, 0)
    vrefs = [vsib, vone, vone, vtwo, vtwo, vone_s, vone_s, vtwo_s]
    for index, slot in enumerate(slots):

        @pl.when(allowed[index])
        def _():
            tile(index + 1, vrefs[index], slot[1] * heads * HD)

    for h in range(heads):
        part = slice(HD * h, HD * h + HD)
        acc[part, :] = acc[part, :] / st_ref[heads + h : heads + h + 1, :]
    rows_ref[...] = jnp.transpose(acc[...])
    half = length // 2
    mine = lax.axis_index("head")
    keep_ref[...] = rows_ref[pl.ds(pl.multiple_of(mine * half, half), half), :].astype(BF16)
    send_ref[...] = rows_ref[pl.ds(pl.multiple_of((1 - mine) * half, half), half), :].astype(BF16)


def grad_body(
    chips, reach_ref, own, sib, one, two, one_s, two_s, g0, gsib, gone, gtwo, gone_s, gtwo_s,
    st, ssib, sone, stwo, sone_s, stwo_s, out_ref, acc,
):
    length = own.shape[0] - REACH_ROWS
    heads = own.shape[1] // HD
    keys = [head_keys(own, length, h) for h in range(heads)]
    low = lax.broadcasted_iota(jnp.int32, (length, 128), 1) < HD

    def tile(ref, row, gref, grow, sref, srow, masked):
        for g in range(heads // 2):
            lanes = slice(128 * g, 128 * g + 128)
            grads = gref[grow : grow + length, lanes]
            far = ref[row : row + length, lanes]
            parts = []
            for h in (2 * g, 2 * g + 1):
                scores = dot_nt(keys[h], far)
                if masked:
                    scores = off_diagonal(scores, 0, 0)
                weights = jnp.exp(scores - sref[srow + h : srow + h + 1, :]).astype(BF16)
                zero = jnp.zeros_like(grads)
                some = jnp.where(low, grads, zero) if h % 2 == 0 else jnp.where(low, zero, grads)
                parts.append(dot_nn(weights, some))
            if masked:
                acc[:, lanes] = parts[0] + parts[1]
            else:
                acc[:, lanes] += parts[0] + parts[1]

    slots = far_slots(chips, sib, one, two, one_s, two_s)
    allowed = allowed_slots(reach_ref, slots, length)
    tile(own, 0, g0, 0, st, 0, True)
    grefs = [gsib, gone, gone, gtwo, gtwo, gone_s, gone_s, gtwo_s]
    srefs = [ssib, sone, sone, stwo, stwo, sone_s, sone_s, stwo_s]
    for index, slot in enumerate(slots):

        @pl.when(allowed[index])
        def _():
            block = slot[1]
            row = block * (length + REACH_ROWS)
            tile(slot[0], row, grefs[index], block * length, srefs[index], 2 * heads * block, False)

    out_ref[...] = acc[...].astype(BF16)


def join_body(own_ref, sib_ref, out_ref):
    rows = own_ref.shape[0]
    out_ref[0:rows, :] = own_ref[...]
    out_ref[rows:, :] = sib_ref[...]


def final_body(chips, reach_ref, keep_ref, got_ref, near_ref, far_ref, *refs):
    *grad_refs, mixed_out, grad_out, acc, mixed, grad, sems = refs
    total = dot_nn(keep_ref[...], near_ref[...]) + dot_nn(got_ref[...], far_ref[...])
    mixed[...] = total.astype(BF16)
    first = pltpu.make_async_copy(mixed, mixed_out, sems.at[0])
    first.start()
    grad_body(chips, reach_ref, *grad_refs, grad, acc)
    second = pltpu.make_async_copy(grad, grad_out, sems.at[1])
    second.start()
    first.wait()
    second.wait()


VMEM = pl.BlockSpec(memory_space=pltpu.VMEM)
SMEM = pl.BlockSpec(memory_space=pltpu.SMEM)


def call(body, args, outs, smem=1, scratch=()):
    specs = [SMEM] * smem + [VMEM] * (len(args) - smem)
    args = [*args[:smem], *(pltpu.with_memory_space_constraint(a, pltpu.VMEM) for a in args[smem:])]
    return pl.pallas_call(
        body,
        in_specs=specs,
        out_specs=[VMEM] * len(outs),
        out_shape=[pltpu.VMEM(shape, dtype) for shape, dtype in outs],
        compiler_params=pltpu.CompilerParams(vmem_limit_bytes=8 * 1024 * 1024),
        scratch_shapes=[pltpu.VMEM(shape, dtype) for shape, dtype in scratch],
    )(*args)


def gathered(own):
    sib = sibling(own)
    rows, width = own.shape
    (both,) = call(join_body, [own, sib], [((2 * rows, width), own.dtype)], smem=0)
    one, two = chip_ring(both, 1), chip_ring(both, 2)
    one, two = lax.optimization_barrier((one, two))
    return [own, sib, one, two, sibling(one), sibling(two)]


def compute(queries, values, scales, block_reach, out_weight, out_grad):
    length, width = queries.shape
    heads = scales.shape[1]
    chips = lax.axis_size("seq") // 2
    keys, turned, grads = pl.pallas_call(
        prepare_body,
        name="prepare",
        in_specs=[SMEM] + [pl.BlockSpec(memory_space=pltpu.HBM)] * 4,
        out_specs=[VMEM] * 3,
        out_shape=[
            pltpu.VMEM((length + REACH_ROWS, width), BF16),
            pltpu.VMEM((width, length), BF16),
            pltpu.VMEM((length, width), BF16),
        ],
        compiler_params=pltpu.CompilerParams(vmem_limit_bytes=8 * 1024 * 1024),
        scratch_shapes=[
            pltpu.VMEM((length, width), BF16),
            pltpu.VMEM((heads, length), F32),
            pltpu.VMEM((length, width), BF16),
            pltpu.SemaphoreType.DMA((4,)),
        ],
    )(block_reach, *(pltpu.with_memory_space_constraint(a, pltpu.HBM) for a in (queries, scales.T, values, out_grad)))
    key_set = gathered(keys)
    value_set = gathered(turned)
    grad_set = gathered(grads)
    far_weight = other_head(out_weight)
    stats, tops, weights = call(
        partial(stats_body, chips),
        [block_reach, *key_set],
        [((2 * heads, length), F32), ((9 * 2 * heads, length), F32), ((9 * heads * length, length), BF16)],
    )
    stat_set = gathered(stats)
    keep, send = call(
        partial(attend_body, chips),
        [block_reach, *key_set, *value_set, stats, tops, weights],
        [((length // 2, width), BF16), ((length // 2, width), BF16)],
        scratch=[((width, length), F32), ((length, width), F32)],
    )
    got = other_head(send)
    half, full = length // 2, out_weight.shape[1]
    inputs = [keep, got, out_weight, far_weight, *key_set, *grad_set, *stat_set]
    inputs = [pltpu.with_memory_space_constraint(a, pltpu.VMEM) for a in inputs]
    mixed, value_grad = pl.pallas_call(
        partial(final_body, chips),
        name="final",
        in_specs=[SMEM] + [VMEM] * len(inputs),
        out_specs=[pl.BlockSpec(memory_space=pltpu.HBM)] * 2,
        out_shape=[
            jax.ShapeDtypeStruct((half, full), BF16),
            jax.ShapeDtypeStruct((length, width), BF16),
        ],
        compiler_params=pltpu.CompilerParams(vmem_limit_bytes=8 * 1024 * 1024),
        scratch_shapes=[
            pltpu.VMEM((length, width), F32),
            pltpu.VMEM((half, full), BF16),
            pltpu.VMEM((length, width), BF16),
            pltpu.SemaphoreType.DMA((2,)),
        ],
    )(block_reach, *inputs)
    return (mixed, value_grad)


def solution(mesh):
    return jax.shard_map(
        compute,
        mesh=mesh,
        in_specs=(
            P("seq", "head"),
            P("seq", "head"),
            P("seq", "head"),
            P("seq"),
            P("head", None),
            P("seq", "head"),
        ),
        out_specs=(P(("seq", "head"), None), P("seq", "head")),
        check_vma=False,
    )
```

```python
from functools import partial

import jax
import jax.numpy as jnp
from jax import lax
from jax.experimental import pallas as pl
from jax.experimental.pallas import tpu as pltpu
from jax.sharding import PartitionSpec as P


HD = 64
NEGATIVE = -1e30
REACH_ROWS = 16
SHIFT_ROWS = 16
LANES = 128
F32 = jnp.float32
BF16 = jnp.bfloat16


def sibling(value):
    count = lax.axis_size("seq")
    return lax.ppermute(value, "seq", [(i, i ^ 1) for i in range(count)])


def chip_ring(value, step):
    chips = lax.axis_size("seq") // 2
    pairs = []
    for chip in range(chips):
        up, down = chip + step, chip - step
        pairs.append((2 * chip, 2 * up if up < chips else 2 * chip + 1))
        pairs.append((2 * chip + 1, 2 * down + 1 if down >= 0 else 2 * chip))
    return lax.ppermute(value, "seq", pairs)


def other_head(value):
    return lax.ppermute(value, "head", [(0, 1), (1, 0)])


def dot_nt(a, b):
    return lax.dot_general(a, b, (((1,), (1,)), ((), ())), preferred_element_type=F32)


def dot_nn(a, b):
    return lax.dot_general(a, b, (((1,), (0,)), ((), ())), preferred_element_type=F32)


def prepare_body(
    reach_ref, q_in, s_in, v_in, g_in, k_ref, vt_ref, gt_ref, q_ref, s_ref, v_ref, g_ref, sems
):
    length, width = q_ref.shape
    pairs = ((q_in, q_ref), (s_in, s_ref), (v_in, v_ref), (g_in, g_ref))
    copies = [pltpu.make_async_copy(a, b, sems.at[i]) for i, (a, b) in enumerate(pairs)]
    for copy in copies:
        copy.start()
    copies[0].wait()
    copies[1].wait()
    low = lax.broadcasted_iota(jnp.int32, (length, LANES), 1) < HD
    scales = jnp.transpose(s_ref[...])
    for g in range(width // LANES):
        lanes = slice(LANES * g, LANES * g + LANES)
        q = q_ref[:, lanes].astype(F32)
        square = q * q
        sum_low = jnp.sum(jnp.where(low, square, 0.0), axis=1, keepdims=True)
        sum_high = jnp.sum(jnp.where(low, 0.0, square), axis=1, keepdims=True)
        inverse = jnp.where(low, lax.rsqrt(sum_low + 1e-6), lax.rsqrt(sum_high + 1e-6))
        scale = jnp.where(low, scales[:, 2 * g : 2 * g + 1], scales[:, 2 * g + 1 : 2 * g + 2])
        k_ref[0:length, lanes] = ((q * inverse) * scale).astype(BF16)
    reach = jnp.full((REACH_ROWS, width), reach_ref[0].astype(F32), F32)
    k_ref[length:, :] = reach.astype(BF16)
    copies[2].wait()
    vt_ref[...] = jnp.transpose(v_ref[...].astype(F32)).astype(BF16)
    copies[3].wait()
    gt_ref[...] = jnp.transpose(g_ref[...].astype(F32)).astype(BF16)


def join_body(*refs):
    *parts, out_ref = refs
    at = 0
    for ref in parts:
        out_ref[at : at + ref.shape[0], :] = ref[...]
        at += ref.shape[0]


def head_keys(k_ref, length, h):
    g = h // 2
    lane = lax.broadcasted_iota(jnp.int32, (length, LANES), 1)
    keep = (lane < HD) if h % 2 == 0 else (lane >= HD)
    rows = k_ref[0:length, LANES * g : LANES * g + LANES]
    return jnp.where(keep, rows, jnp.zeros_like(rows))


NEAR = ((0, 0, 0, None), (1, 0, 1, None))
DIRECT = ((0, 0, 2, 1), (0, 1, 1, 1), (1, 0, 4, 2), (1, 1, 3, 2))
PASSED = ((0, 0, 3, -1), (0, 1, 2, -1), (1, 1, 4, -2))


def allowed_slots(chips, reach_ref, slots, keys, length):
    place = lax.axis_index("seq")
    chip, toward = lax.div(place, 2), 2 * lax.rem(place, 2) - 1
    near = reach_ref[0].astype(F32)
    result = []
    for index, block, distance, away in slots:
        if distance == 0:
            result.append(None)
            continue
        start = block * (length + REACH_ROWS) + length
        far = jnp.max(keys[index][start : start + REACH_ROWS, 0:LANES].astype(F32))
        allowed = jnp.minimum(near, far) >= float(distance)
        if away is not None:
            other = chip + away * toward
            allowed = jnp.logical_and(allowed, jnp.logical_and(other >= 0, other < chips))
        result.append(allowed)
    return result


def off_diagonal(scores, row, column):
    rows = lax.broadcasted_iota(jnp.int32, scores.shape, 0) + row
    columns = lax.broadcasted_iota(jnp.int32, scores.shape, 1) + column
    return jnp.where(rows == columns, NEGATIVE, scores)


def stats_body(chips, slots, reach_ref, own, *refs):
    count = len({slot[0] for slot in slots})
    keys, rest = refs[:count], refs[count:]
    length = own.shape[0] - REACH_ROWS
    heads = own.shape[1] // HD
    last = slots is PASSED
    if last:
        near_ref, direct_ref, m_ref, w_ref, total_ref, f_ref, shift_ref = rest
    else:
        m_ref, w_ref = rest
    mine = [head_keys(own, length, h) for h in range(heads)]

    def tile(index):
        array, block, distance, _ = slots[index]
        row = block * (length + REACH_ROWS)
        products = []
        for g in range(heads // 2):
            rows = keys[array][row : row + length, LANES * g : LANES * g + LANES]
            for part in range(0, length, LANES):
                pair = [mine[h][part : part + LANES, :] for h in (2 * g, 2 * g + 1)]
                products.append((g, part, dot_nt(rows, jnp.concatenate(pair, axis=0))))
        for g, part, product in products:
            for h in (2 * g, 2 * g + 1):
                scores = product[:, LANES * (h % 2) : LANES * (h % 2) + LANES]
                if distance == 0:
                    scores = off_diagonal(scores, 0, part)
                top = jnp.max(scores, axis=0, keepdims=True)
                exponent = jnp.exp(scores - top)
                total = jnp.sum(exponent, axis=0, keepdims=True)
                lanes = slice(part, part + LANES)
                at = 2 * heads * index + h
                m_ref[at : at + 1, lanes] = top
                m_ref[at + heads : at + heads + 1, lanes] = total
                at = (index * heads + h) * length * (length // LANES) + part // LANES * length
                w_ref[at : at + length, :] = exponent.astype(BF16)

    allowed = allowed_slots(chips, reach_ref, slots, keys, length)
    for index, ok in enumerate(allowed):
        if ok is None:
            tile(index)
            continue
        at = 2 * heads * index
        m_ref[at : at + heads, :] = jnp.full((heads, length), NEGATIVE, F32)
        m_ref[at + heads : at + 2 * heads, :] = jnp.zeros((heads, length), F32)
        pl.when(ok)(partial(tile, index))

    if last:
        parts = []
        for ref, part in ((near_ref, NEAR), (direct_ref, DIRECT), (m_ref, PASSED)):
            parts += [(ref, 2 * heads * s) for s in range(len(part))]
        tops = [ref[at : at + heads, :] for ref, at in parts]
        top = tops[0]
        for other in tops[1:]:
            top = jnp.maximum(top, other)
        total = jnp.zeros((heads, length), F32)
        for index, (ref, at) in enumerate(parts):
            factor = jnp.exp(tops[index] - top)
            total = total + factor * ref[at + heads : at + 2 * heads, :]
            f_ref[2 * heads * index : 2 * heads * index + heads, :] = factor
        left = top + jnp.log(total)
        terms = []
        for _ in range(3):
            term = left.astype(BF16).astype(F32)
            terms.append(term)
            left = left - term
        terms.append(jnp.zeros((SHIFT_ROWS - 3 * heads, length), F32))
        shift_ref[...] = jnp.concatenate(terms, axis=0).astype(BF16)
        total_ref[...] = total


def attend_body(chips, slots, reach_ref, *refs):
    count = len({slot[0] for slot in slots})
    keys, values, rest = refs[:count], refs[count : 2 * count], refs[2 * count :]
    first, last = slots is NEAR, slots is PASSED
    before = {NEAR: 0, DIRECT: len(NEAR), PASSED: len(NEAR) + len(DIRECT)}[slots]
    if first:
        w_ref, f_ref, acc = rest
    elif last:
        w_ref, f_ref, total_ref, acc_in, keep_ref, send_ref, acc, rows_ref = rest
    else:
        w_ref, f_ref, acc_in, acc = rest
    length = acc.shape[1]
    heads = acc.shape[0] // HD
    if not first:
        acc[...] = acc_in[...]

    def tile(index):
        array, block, distance, _ = slots[index]
        for h in range(heads):
            at = (index * heads + h) * length * (length // LANES)
            starts = range(at, at + length * (length // LANES), length)
            weights = [w_ref[start : start + length, :] for start in starts]
            row = (block * heads + h) * HD
            numer = dot_nn(values[array][row : row + HD, :], jnp.concatenate(weights, axis=1))
            at = 2 * heads * (before + index) + h
            numer = numer * f_ref[at : at + 1, :]
            part = slice(HD * h, HD * h + HD)
            if distance == 0:
                acc[part, :] = numer
            else:
                acc[part, :] += numer

    for index, ok in enumerate(allowed_slots(chips, reach_ref, slots, keys, length)):
        if ok is None:
            tile(index)
        else:
            pl.when(ok)(partial(tile, index))

    if last:
        for h in range(heads):
            part = slice(HD * h, HD * h + HD)
            acc[part, :] = acc[part, :] / total_ref[h : h + 1, :]
        rows_ref[...] = jnp.transpose(acc[...])
        half = length // 2
        mine = lax.axis_index("head")
        keep_ref[...] = rows_ref[pl.ds(pl.multiple_of(mine * half, half), half), :].astype(BF16)
        other = pl.multiple_of((1 - mine) * half, half)
        send_ref[...] = rows_ref[pl.ds(other, half), :].astype(BF16)


def grad_tiles(chips, slots, reach_ref, own, keys, grads, shifts, acc):
    length = own.shape[0] - REACH_ROWS
    heads = own.shape[1] // HD
    lane = lax.broadcasted_iota(jnp.int32, (length, LANES), 1)
    low = lane < HD
    mine = []
    for h in range(heads):
        base = HD if h % 2 == 0 else 0
        term = lane - (base + h)
        one = jnp.logical_or(term == 0, jnp.logical_or(term == heads, term == 2 * heads))
        minus = jnp.where(one, -1.0, 0.0).astype(BF16)
        rows = own[0:length, LANES * (h // 2) : LANES * (h // 2) + LANES]
        mine.append(jnp.where(low if h % 2 == 0 else ~low, rows, minus))

    def tile(index):
        array, block, distance, _ = slots[index]
        row = block * (length + REACH_ROWS)
        ref, grow, srow = grads[array], block * heads * HD, block * SHIFT_ROWS
        terms = shifts[array][srow : srow + SHIFT_ROWS, :].astype(F32)
        rest = jnp.zeros((HD - SHIFT_ROWS, length), F32)
        terms = jnp.transpose(jnp.concatenate([terms, rest, terms, rest], axis=0)).astype(BF16)
        products = []
        for h in range(heads):
            g = h // 2
            far = keys[array][row : row + length, LANES * g : LANES * g + LANES]
            far = jnp.where(low if h % 2 == 0 else ~low, far, terms)
            products.append(dot_nt(far, mine[h]))
        weights = []
        for h in range(heads):
            scores = products[h]
            if distance == 0:
                scores = off_diagonal(scores, 0, 0)
            weights.append(jnp.exp(scores).astype(BF16))
        for h in range(heads):
            part = slice(HD * h, HD * h + HD)
            share = dot_nn(ref[grow + HD * h : grow + HD * h + HD, :], weights[h])
            if distance == 0:
                acc[part, :] = share
            else:
                acc[part, :] += share

    for index, ok in enumerate(allowed_slots(chips, reach_ref, slots, keys, length)):
        if ok is None:
            tile(index)
        else:
            pl.when(ok)(partial(tile, index))


def grad_body(chips, slots, reach_ref, own, *refs):
    keys, grads, shifts, rest = refs[0:2], refs[2:4], refs[4:6], refs[6:]
    acc = rest[-1]
    if slots is not NEAR:
        acc[...] = rest[0][...]
    grad_tiles(chips, slots, reach_ref, own, keys, grads, shifts, acc)


def final_body(chips, reach_ref, keep_ref, got_ref, near_ref, far_ref, *refs):
    own, acc_in, *refs = refs
    keys, grads, shifts, rest = refs[0:2], refs[2:4], refs[4:6], refs[6:]
    mixed_out, grad_out, acc, mixed, grad, sems = rest
    total = dot_nn(keep_ref[...], near_ref[...]) + dot_nn(got_ref[...], far_ref[...])
    mixed[...] = total.astype(BF16)
    first = pltpu.make_async_copy(mixed, mixed_out, sems.at[0])
    first.start()
    acc[...] = acc_in[...]
    grad_tiles(chips, PASSED, reach_ref, own, keys, grads, shifts, acc)
    grad[...] = jnp.transpose(acc[...]).astype(BF16)
    second = pltpu.make_async_copy(grad, grad_out, sems.at[1])
    second.start()
    first.wait()
    second.wait()


VMEM = pl.BlockSpec(memory_space=pltpu.VMEM)
SMEM = pl.BlockSpec(memory_space=pltpu.SMEM)
HBM = pl.BlockSpec(memory_space=pltpu.HBM)
PARAMS = pltpu.CompilerParams(vmem_limit_bytes=8 * 1024 * 1024)


def call(body, scalars, args, outs, scratch=()):
    args = [pltpu.with_memory_space_constraint(a, pltpu.VMEM) for a in args]
    run = pl.pallas_call(
        body,
        in_specs=[SMEM] * len(scalars) + [VMEM] * len(args),
        out_specs=[VMEM] * len(outs),
        out_shape=[pltpu.VMEM(shape, dtype) for shape, dtype in outs],
        compiler_params=PARAMS,
        scratch_shapes=[pltpu.VMEM(shape, dtype) for shape, dtype in scratch],
    )
    return list(run(*scalars, *args))


def joined(parts):
    rows, width = sum(part.shape[0] for part in parts), parts[0].shape[1]
    (both,) = call(join_body, [], parts, [((rows, width), BF16)])
    return both


def gathered(own):
    sib = sibling(own)
    return [own, sib], *rings(joined([own, sib]))


def rings(both):
    one, two = chip_ring(both, 1), chip_ring(both, 2)
    one, two = lax.optimization_barrier((one, two))
    return [one, two], [sibling(one), sibling(two)]


def compute(queries, values, scales, block_reach, out_weight, out_grad):
    length, width = queries.shape
    heads = scales.shape[1]
    chips = lax.axis_size("seq") // 2
    inputs = [queries, scales.T, values, out_grad]
    keys, turned, grads = pl.pallas_call(
        prepare_body,
        name="prepare",
        in_specs=[SMEM] + [HBM] * 4,
        out_specs=[VMEM] * 3,
        out_shape=[
            pltpu.VMEM((length + REACH_ROWS, width), BF16),
            pltpu.VMEM((width, length), BF16),
            pltpu.VMEM((width, length), BF16),
        ],
        compiler_params=PARAMS,
        scratch_shapes=[
            pltpu.VMEM((length, width), BF16),
            pltpu.VMEM((heads, length), F32),
            pltpu.VMEM((length, width), BF16),
            pltpu.VMEM((length, width), BF16),
            pltpu.SemaphoreType.DMA((4,)),
        ],
    )(block_reach, *(pltpu.with_memory_space_constraint(a, pltpu.HBM) for a in inputs))
    stages = (NEAR, DIRECT, PASSED)
    key_set = gathered(keys)
    value_set = gathered(turned)
    grad_set = gathered(grads)
    far_weight = other_head(out_weight)

    tops, weights = [], []
    for index, slots in enumerate(stages):
        last = slots is PASSED
        outs = [
            ((2 * heads * len(slots), length), F32),
            ((heads * len(slots) * length * length // LANES, LANES), BF16),
        ]
        if last:
            total = sum(len(part) for part in stages)
            outs += [((heads, length), F32), ((2 * heads * total, length), F32)]
            outs += [((SHIFT_ROWS, length), BF16)]
        args = [keys, *key_set[index], *(tops if last else [])]
        body = partial(stats_body, chips, slots)
        top, weight, *rest = call(body, [block_reach], args, outs)
        tops.append(top)
        weights.append(weight)
    totals, factors, shifts = rest
    shift_set = gathered(shifts)

    running = []
    for index, slots in enumerate(stages):
        args = [*key_set[index], *value_set[index], weights[index], factors]
        body = partial(attend_body, chips, slots)
        if slots is PASSED:
            args += [totals, *running]
            outs = [((length // 2, width), BF16)] * 2
            scratch = [((width, length), F32), ((length, width), F32)]
            keep, send = call(body, [block_reach], args, outs, scratch)
        else:
            running = call(body, [block_reach], args + running, [((width, length), F32)])
    got = other_head(send)

    running = []
    for index, slots in enumerate(stages[:2]):
        args = [keys, *key_set[index], *grad_set[index], *shift_set[index], *running]
        body = partial(grad_body, chips, slots)
        running = call(body, [block_reach], args, [((width, length), F32)])
    half, full = length // 2, out_weight.shape[1]
    inputs = [keep, got, out_weight, far_weight, keys, *running]
    inputs += [*key_set[2], *grad_set[2], *shift_set[2]]
    inputs = [pltpu.with_memory_space_constraint(a, pltpu.VMEM) for a in inputs]
    mixed, value_grad = pl.pallas_call(
        partial(final_body, chips),
        name="final",
        in_specs=[SMEM] + [VMEM] * len(inputs),
        out_specs=[HBM] * 2,
        out_shape=[
            jax.ShapeDtypeStruct((half, full), BF16),
            jax.ShapeDtypeStruct((length, width), BF16),
        ],
        compiler_params=PARAMS,
        scratch_shapes=[
            pltpu.VMEM((width, length), F32),
            pltpu.VMEM((half, full), BF16),
            pltpu.VMEM((length, width), BF16),
            pltpu.SemaphoreType.DMA((2,)),
        ],
    )(block_reach, *inputs)
    return (mixed, value_grad)


def solution(mesh):
    return jax.shard_map(
        compute,
        mesh=mesh,
        in_specs=(
            P("seq", "head"),
            P("seq", "head"),
            P("seq", "head"),
            P("seq"),
            P("head", None),
            P("seq", "head"),
        ),
        out_specs=(P(("seq", "head"), None), P("seq", "head")),
        check_vma=False,
    )
```

```python
from functools import partial

import jax
import jax.numpy as jnp
from jax import lax
from jax.experimental import pallas as pl
from jax.experimental.pallas import tpu as pltpu
from jax.sharding import PartitionSpec as P


HD = 64
NEGATIVE = -1e30
REACH_ROWS = 16
SHIFT_ROWS = 16
LANES = 128
F32 = jnp.float32
BF16 = jnp.bfloat16


def sibling(value):
    count = lax.axis_size("seq")
    return lax.ppermute(value, "seq", [(i, i ^ 1) for i in range(count)])


def chip_ring(value, step):
    chips = lax.axis_size("seq") // 2
    pairs = []
    for chip in range(chips):
        up, down = chip + step, chip - step
        pairs.append((2 * chip, 2 * up if up < chips else 2 * chip + 1))
        pairs.append((2 * chip + 1, 2 * down + 1 if down >= 0 else 2 * chip))
    return lax.ppermute(value, "seq", pairs)


def other_head(value):
    return lax.ppermute(value, "head", [(0, 1), (1, 0)])


def dot_nt(a, b):
    return lax.dot_general(a, b, (((1,), (1,)), ((), ())), preferred_element_type=F32)


def dot_nn(a, b):
    return lax.dot_general(a, b, (((1,), (0,)), ((), ())), preferred_element_type=F32)


def split_terms(value, count):
    terms = []
    for _ in range(count):
        terms.append(value.astype(BF16).astype(F32))
        value = value - terms[-1]
    return terms


def prepare_body(reach_ref, q_in, s_in, v_in, g_in, k_ref, v_ref, g_ref, q_ref, s_ref, sems):
    length, width = q_ref.shape
    pairs = ((q_in, q_ref), (s_in, s_ref), (v_in, v_ref), (g_in, g_ref))
    copies = [pltpu.make_async_copy(a, b, sems.at[i]) for i, (a, b) in enumerate(pairs)]
    for copy in copies:
        copy.start()
    copies[0].wait()
    copies[1].wait()
    row = lax.broadcasted_iota(jnp.int32, (LANES, LANES), 0)
    lane = lax.broadcasted_iota(jnp.int32, (LANES, LANES), 1)
    same = jnp.where(lax.div(row, HD) == lax.div(lane, HD), 1.0, 0.0).astype(BF16)
    scale_terms = split_terms(s_ref[...], 3)
    scale_terms.append(jnp.zeros((LANES - 3 * s_ref.shape[0], length), F32))
    scale_terms = jnp.transpose(jnp.concatenate(scale_terms, axis=0)).astype(BF16)
    for g in range(width // LANES):
        lanes = slice(LANES * g, LANES * g + LANES)
        q = q_ref[:, lanes].astype(F32)
        high, rest = split_terms(q * q, 2)
        total = dot_nn(high.astype(BF16), same) + dot_nn(rest.astype(BF16), same)
        head = 2 * g + lax.div(lane, HD)
        pick = jnp.where(lax.rem(row, s_ref.shape[0]) == head, 1.0, 0.0)
        pick = jnp.where(row < 3 * s_ref.shape[0], pick, 0.0).astype(BF16)
        scale = dot_nn(scale_terms, pick)
        k_ref[0:length, lanes] = ((q * lax.rsqrt(total + 1e-6)) * scale).astype(BF16)
    reach = jnp.full((REACH_ROWS, width), reach_ref[0].astype(F32), F32)
    k_ref[length:, :] = reach.astype(BF16)
    copies[2].wait()
    copies[3].wait()


def turn_body(v_ref, g_ref, vt_ref, gt_ref):
    vt_ref[...] = jnp.transpose(v_ref[...].astype(F32)).astype(BF16)
    gt_ref[...] = jnp.transpose(g_ref[...].astype(F32)).astype(BF16)


def join_body(*refs):
    *parts, out_ref = refs
    at = 0
    for ref in parts:
        out_ref[at : at + ref.shape[0], :] = ref[...]
        at += ref.shape[0]


def head_keys(k_ref, length, h):
    g = h // 2
    lane = lax.broadcasted_iota(jnp.int32, (length, LANES), 1)
    keep = (lane < HD) if h % 2 == 0 else (lane >= HD)
    rows = k_ref[0:length, LANES * g : LANES * g + LANES]
    return jnp.where(keep, rows, jnp.zeros_like(rows))


NEAR = ((0, 0, 0, None), (1, 0, 1, None))
DIRECT = ((0, 0, 2, 1), (0, 1, 1, 1), (1, 0, 4, 2), (1, 1, 3, 2))
SIBLING = ((0, 0, 1, None),)
PASSED = ((0, 0, 3, -1), (0, 1, 2, -1), (1, 1, 4, -2))


def allowed_slots(chips, reach_ref, slots, keys, length):
    place = lax.axis_index("seq")
    chip, toward = lax.div(place, 2), 2 * lax.rem(place, 2) - 1
    near = reach_ref[0].astype(F32)
    result = []
    for index, block, distance, away in slots:
        if distance == 0:
            result.append(None)
            continue
        start = block * (length + REACH_ROWS) + length
        far = jnp.max(keys[index][start : start + REACH_ROWS, 0:LANES].astype(F32))
        allowed = jnp.minimum(near, far) >= float(distance)
        if away is not None:
            other = chip + away * toward
            allowed = jnp.logical_and(allowed, jnp.logical_and(other >= 0, other < chips))
        result.append(allowed)
    return result


def off_diagonal(scores, row, column):
    rows = lax.broadcasted_iota(jnp.int32, scores.shape, 0) + row
    columns = lax.broadcasted_iota(jnp.int32, scores.shape, 1) + column
    return jnp.where(rows == columns, NEGATIVE, scores)


def stats_body(chips, slots, reach_ref, own, *refs):
    *refs, ok_ref = refs
    count = len({slot[0] for slot in slots})
    keys, rest = refs[:count], refs[count:]
    length = own.shape[0] - REACH_ROWS
    heads = own.shape[1] // HD
    last = slots is PASSED
    if last:
        near_ref, direct_ref, m_ref, w_ref, total_ref, f_ref, shift_ref = rest
    else:
        m_ref, w_ref = rest
    mine = [head_keys(own, length, h) for h in range(heads)]

    def tile(index):
        array, block, distance, _ = slots[index]
        row = block * (length + REACH_ROWS)
        products = []
        for g in range(heads // 2):
            rows = keys[array][row : row + length, LANES * g : LANES * g + LANES]
            for part in range(0, length, LANES):
                pair = [mine[h][part : part + LANES, :] for h in (2 * g, 2 * g + 1)]
                products.append((g, part, dot_nt(rows, jnp.concatenate(pair, axis=0))))
        for g, part, product in products:
            for h in (2 * g, 2 * g + 1):
                scores = product[:, LANES * (h % 2) : LANES * (h % 2) + LANES]
                if distance == 0:
                    scores = off_diagonal(scores, 0, part)
                top = jnp.max(scores, axis=0, keepdims=True)
                exponent = jnp.exp(scores - top)
                total = jnp.sum(exponent, axis=0, keepdims=True)
                lanes = slice(part, part + LANES)
                at = 2 * heads * index + h
                m_ref[at : at + 1, lanes] = top
                m_ref[at + heads : at + heads + 1, lanes] = total
                at = (index * heads + h) * length * (length // LANES) + part // LANES * length
                w_ref[at : at + length, :] = exponent.astype(BF16)

    allowed = allowed_slots(chips, reach_ref, slots, keys, length)
    for index, ok in enumerate(allowed):
        if ok is None:
            ok_ref[index] = 1
            tile(index)
            continue
        ok_ref[index] = ok.astype(jnp.int32)
        at = 2 * heads * index
        m_ref[at : at + heads, :] = jnp.full((heads, length), NEGATIVE, F32)
        m_ref[at + heads : at + 2 * heads, :] = jnp.zeros((heads, length), F32)
        pl.when(ok)(partial(tile, index))

    if last:
        parts = []
        for ref, part in ((near_ref, NEAR), (direct_ref, DIRECT), (m_ref, PASSED)):
            parts += [(ref, 2 * heads * s) for s in range(len(part))]
        tops = [ref[at : at + heads, :] for ref, at in parts]
        top = tops[0]
        for other in tops[1:]:
            top = jnp.maximum(top, other)
        total = jnp.zeros((heads, length), F32)
        for index, (ref, at) in enumerate(parts):
            factor = jnp.exp(tops[index] - top)
            total = total + factor * ref[at + heads : at + 2 * heads, :]
            f_ref[2 * heads * index : 2 * heads * index + heads, :] = factor
        terms = split_terms(top + jnp.log(total), 3)
        terms.append(jnp.zeros((SHIFT_ROWS - 3 * heads, length), F32))
        shift_ref[...] = jnp.concatenate(terms, axis=0).astype(BF16)
        total_ref[...] = total


def numerator(values, w_ref, slots, index, h, length, heads):
    array, block, _, _ = slots[index]
    at = (index * heads + h) * length * (length // LANES)
    starts = range(at, at + length * (length // LANES), length)
    weights = [w_ref[start : start + length, :] for start in starts]
    row = (block * heads + h) * HD
    return dot_nn(values[array][row : row + HD, :], jnp.concatenate(weights, axis=1))


def attend_near_body(own, sib, w_ref, *outs):
    width, length = outs[0].shape
    heads = width // HD
    for index, out in enumerate(outs):
        for h in range(heads):
            part = numerator((own, sib), w_ref, NEAR, index, h, length, heads)
            out[HD * h : HD * h + HD, :] = part


def attend_body(slots, ok_ref, *refs):
    values, refs = refs[0:2], refs[2:]
    last = slots is PASSED
    if last:
        w_ref, f_ref, total_ref, acc_in, keep_ref, send_ref, acc, rows_ref = refs
    else:
        ok_sib, values, refs = values[0], (values[1], refs[0]), refs[1:]
        w_ref, f_ref, own_in, sib_in, acc = refs
    width, length = acc.shape
    heads = width // HD
    before = len(NEAR) + (len(DIRECT) if last else 0)

    def factor(slot, h):
        at = 2 * heads * slot + h
        return f_ref[at : at + 1, :]

    def tile(index):
        for h in range(heads):
            numer = numerator(values, w_ref, slots, index, h, length, heads)
            acc[HD * h : HD * h + HD, :] += numer * factor(before + index, h)

    def near():
        for h in range(heads):
            part = slice(HD * h, HD * h + HD)
            acc[part, :] += sib_in[part, :] * factor(1, h)

    if last:
        acc[...] = acc_in[...]
    else:
        for h in range(heads):
            part = slice(HD * h, HD * h + HD)
            acc[part, :] = own_in[part, :] * factor(0, h)
        pl.when(ok_sib[1] > 0)(near)
    for index in range(len(slots)):
        pl.when(ok_ref[index] > 0)(partial(tile, index))
    if last:
        for h in range(heads):
            part = slice(HD * h, HD * h + HD)
            acc[part, :] = acc[part, :] / total_ref[h : h + 1, :]
        rows_ref[...] = jnp.transpose(acc[...])
        half = length // 2
        mine = lax.axis_index("head")
        keep_ref[...] = rows_ref[pl.ds(pl.multiple_of(mine * half, half), half), :].astype(BF16)
        other = pl.multiple_of((1 - mine) * half, half)
        send_ref[...] = rows_ref[pl.ds(other, half), :].astype(BF16)


def shifted_keys(own, length, heads):
    lane = lax.broadcasted_iota(jnp.int32, (length, LANES), 1)
    result = []
    for h in range(heads):
        term = lane - ((HD if h % 2 == 0 else 0) + h)
        one = jnp.logical_or(term == 0, jnp.logical_or(term == heads, term == 2 * heads))
        minus = jnp.where(one, -1.0, 0.0).astype(BF16)
        rows = own[0:length, LANES * (h // 2) : LANES * (h // 2) + LANES]
        result.append(jnp.where((lane < HD) if h % 2 == 0 else (lane >= HD), rows, minus))
    return result


def shift_terms(ref, block, length):
    terms = ref[block * SHIFT_ROWS : (block + 1) * SHIFT_ROWS, :].astype(F32)
    rest = jnp.zeros((HD - SHIFT_ROWS, length), F32)
    return jnp.transpose(jnp.concatenate([terms, rest, terms, rest], axis=0)).astype(BF16)


def grad_tile(mine, key, grad, terms, block, length, width, heads, acc, own):
    low = lax.broadcasted_iota(jnp.int32, (length, LANES), 1) < HD
    row = block * (length + REACH_ROWS)
    products = []
    for h in heads:
        far = key[row : row + length, LANES * (h // 2) : LANES * (h // 2) + LANES]
        far = jnp.where(low if h % 2 == 0 else ~low, far, terms)
        products.append(dot_nt(far, mine[h]))
    if own:
        products = [off_diagonal(scores, 0, 0) for scores in products]
    weights = [jnp.exp(scores).astype(BF16) for scores in products]
    for h, weight in zip(heads, weights):
        part = slice(HD * h, HD * h + HD)
        share = dot_nn(grad[block * width + HD * h : block * width + HD * h + HD, :], weight)
        if own:
            acc[part, :] = share
        else:
            acc[part, :] += share


def grad_own_body(key, grad, shift, acc):
    width, length = acc.shape
    heads = range(width // HD)
    mine = shifted_keys(key, length, width // HD)
    terms = shift_terms(shift, 0, length)
    grad_tile(mine, key, grad, terms, 0, length, width, heads, acc, True)


def grad_body(slots, ok_ref, own, *refs):
    count = len({slot[0] for slot in slots})
    keys, grads, shifts = refs[0:count], refs[count : 2 * count], refs[2 * count : 3 * count]
    acc_in, acc = refs[3 * count :]
    width, length = acc.shape
    heads = range(width // HD)
    mine = shifted_keys(own, length, width // HD)
    acc[...] = acc_in[...]

    def tile(array, block):
        terms = shift_terms(shifts[array], block, length)
        key, grad = keys[array], grads[array]
        grad_tile(mine, key, grad, terms, block, length, width, heads, acc, False)

    for index, (array, block, _, _) in enumerate(slots):
        at = index + (len(NEAR) - 1 if slots is SIBLING else 0)
        pl.when(ok_ref[at] > 0)(partial(tile, array, block))


def final_body(ok_ref, keep_ref, got_ref, near_ref, far_ref, own, acc_in, *refs):
    keys, grads, shifts, rest = refs[0:2], refs[2:4], refs[4:6], refs[6:]
    mixed_out, grad_out, acc, mixed, turned, sems = rest
    width, length = acc.shape
    total = dot_nn(keep_ref[...], near_ref[...]) + dot_nn(got_ref[...], far_ref[...])
    mixed[...] = total.astype(BF16)
    copies = [pltpu.make_async_copy(mixed, mixed_out, sems.at[0])]
    copies[0].start()
    acc[...] = acc_in[...]
    mine = shifted_keys(own, length, width // HD)

    def tile(index):
        array, block, _, _ = PASSED[index]
        heads, terms = range(width // HD), shift_terms(shifts[array], block, length)
        key, grad = keys[array], grads[array]
        grad_tile(mine, key, grad, terms, block, length, width, heads, acc, False)

    for index in range(len(PASSED)):
        pl.when(ok_ref[index] > 0)(partial(tile, index))
    for group in range(width // LANES):
        lanes = slice(LANES * group, LANES * group + LANES)
        turned[group] = jnp.transpose(acc[lanes, :]).astype(BF16)
        copy = pltpu.make_async_copy(turned.at[group], grad_out.at[:, lanes], sems.at[group + 1])
        copy.start()
        copies.append(copy)
    for copy in copies:
        copy.wait()


VMEM = pl.BlockSpec(memory_space=pltpu.VMEM)
SMEM = pl.BlockSpec(memory_space=pltpu.SMEM)
HBM = pl.BlockSpec(memory_space=pltpu.HBM)
PARAMS = pltpu.CompilerParams(vmem_limit_bytes=8 * 1024 * 1024)


def call(body, scalars, args, outs, scratch=(), flags=0):
    args = [pltpu.with_memory_space_constraint(a, pltpu.VMEM) for a in args]
    run = pl.pallas_call(
        body,
        in_specs=[SMEM] * len(scalars) + [VMEM] * len(args),
        out_specs=[VMEM] * len(outs) + [SMEM] * (flags > 0),
        out_shape=[pltpu.VMEM(shape, dtype) for shape, dtype in outs]
        + [pltpu.SMEM((flags,), jnp.int32)] * (flags > 0),
        compiler_params=PARAMS,
        scratch_shapes=[pltpu.VMEM(shape, dtype) for shape, dtype in scratch],
    )
    return list(run(*scalars, *args))


def joined(parts):
    rows, width = sum(part.shape[0] for part in parts), parts[0].shape[1]
    (both,) = call(join_body, [], parts, [((rows, width), BF16)])
    return both


def gathered(own):
    sib = sibling(own)
    return [own, sib], *rings(joined([own, sib]))


def rings(both):
    one, two = chip_ring(both, 1), chip_ring(both, 2)
    one, two = lax.optimization_barrier((one, two))
    return [one, two], [sibling(one), sibling(two)]


def compute(queries, values, scales, block_reach, out_weight, out_grad):
    length, width = queries.shape
    heads = scales.shape[1]
    chips = lax.axis_size("seq") // 2
    inputs = [queries, scales.T, values, out_grad]
    keys, *raw = pl.pallas_call(
        prepare_body,
        name="prepare",
        in_specs=[SMEM] + [HBM] * 4,
        out_specs=[VMEM] * 3,
        out_shape=[
            pltpu.VMEM((length + REACH_ROWS, width), BF16),
            pltpu.VMEM((length, width), BF16),
            pltpu.VMEM((length, width), BF16),
        ],
        compiler_params=PARAMS,
        scratch_shapes=[
            pltpu.VMEM((length, width), BF16),
            pltpu.VMEM((heads, length), F32),
            pltpu.SemaphoreType.DMA((4,)),
        ],
    )(block_reach, *(pltpu.with_memory_space_constraint(a, pltpu.HBM) for a in inputs))
    turned, grads = call(turn_body, [], raw, [((width, length), BF16)] * 2)
    stages = (NEAR, DIRECT, PASSED)
    key_set = gathered(keys)
    value_set = gathered(turned)
    grad_set = gathered(grads)
    far_weight = other_head(out_weight)

    tops, weights, allowed = [], [], []
    for index, slots in enumerate(stages):
        last = slots is PASSED
        outs = [
            ((2 * heads * len(slots), length), F32),
            ((heads * len(slots) * length * length // LANES, LANES), BF16),
        ]
        if last:
            total = sum(len(part) for part in stages)
            outs += [((heads, length), F32), ((2 * heads * total, length), F32)]
            outs += [((SHIFT_ROWS, length), BF16)]
        args = [keys, *key_set[index], *(tops if last else [])]
        body = partial(stats_body, chips, slots)
        top, weight, *rest, ok = call(body, [block_reach], args, outs, flags=len(slots))
        tops.append(top)
        weights.append(weight)
        allowed.append(ok)
    totals, factors, shifts = rest
    shift_set = gathered(shifts)

    whole = ((width, length), F32)
    near = call(attend_near_body, [], [*value_set[0], weights[0]], [whole] * 2)
    args = [*value_set[1], weights[1], factors, *near]
    (running,) = call(
        lambda ok_sib, ok, *refs: attend_body(DIRECT, ok, ok_sib, *refs),
        [allowed[0], allowed[1]],
        args,
        [whole],
    )
    args = [*value_set[2], weights[2], factors, totals, running]
    outs = [((length // 2, width), BF16)] * 2
    scratch = [whole, ((length, width), F32)]
    body = partial(attend_body, PASSED)
    keep, send = call(body, [allowed[2]], args, outs, scratch)
    got = other_head(send)

    args = [keys, grads, shifts]
    running = call(grad_own_body, [], args, [whole])
    sets = (key_set, grad_set, shift_set)
    args = [keys, *(part[0][1] for part in sets), *running]
    running = call(partial(grad_body, SIBLING), [allowed[0]], args, [whole])
    args = [keys, *key_set[1], *grad_set[1], *shift_set[1], *running]
    (running,) = call(partial(grad_body, DIRECT), [allowed[1]], args, [whole])
    half, full = length // 2, out_weight.shape[1]
    inputs = [keep, got, out_weight, far_weight, keys, running]
    inputs += [*key_set[2], *grad_set[2], *shift_set[2]]
    inputs = [pltpu.with_memory_space_constraint(a, pltpu.VMEM) for a in inputs]
    mixed, value_grad = pl.pallas_call(
        final_body,
        name="final",
        in_specs=[SMEM] + [VMEM] * len(inputs),
        out_specs=[HBM] * 2,
        out_shape=[
            jax.ShapeDtypeStruct((half, full), BF16),
            jax.ShapeDtypeStruct((length, width), BF16),
        ],
        compiler_params=PARAMS,
        scratch_shapes=[
            pltpu.VMEM((width, length), F32),
            pltpu.VMEM((half, full), BF16),
            pltpu.VMEM((width // LANES, length, LANES), BF16),
            pltpu.SemaphoreType.DMA((1 + width // LANES,)),
        ],
    )(allowed[2], *inputs)
    return (mixed, value_grad)


def solution(mesh):
    return jax.shard_map(
        compute,
        mesh=mesh,
        in_specs=(
            P("seq", "head"),
            P("seq", "head"),
            P("seq", "head"),
            P("seq"),
            P("head", None),
            P("seq", "head"),
        ),
        out_specs=(P(("seq", "head"), None), P("seq", "head")),
        check_vma=False,
    )
```

```python
from functools import partial

import jax
import jax.numpy as jnp
from jax import lax
from jax.experimental import pallas as pl
from jax.experimental.pallas import tpu as pltpu
from jax.sharding import PartitionSpec as P


HD = 64
NEGATIVE = -1e30
REACH_ROWS = 16
SHIFT_ROWS = 16
LANES = 128
F32 = jnp.float32
BF16 = jnp.bfloat16


def sibling(value):
    count = lax.axis_size("seq")
    return lax.ppermute(value, "seq", [(i, i ^ 1) for i in range(count)])


def chip_ring(value, step):
    chips = lax.axis_size("seq") // 2
    pairs = []
    for chip in range(chips):
        up, down = chip + step, chip - step
        pairs.append((2 * chip, 2 * up if up < chips else 2 * chip + 1))
        pairs.append((2 * chip + 1, 2 * down + 1 if down >= 0 else 2 * chip))
    return lax.ppermute(value, "seq", pairs)


def other_head(value):
    return lax.ppermute(value, "head", [(0, 1), (1, 0)])


def dot_nt(a, b):
    return lax.dot_general(a, b, (((1,), (1,)), ((), ())), preferred_element_type=F32)


def dot_nn(a, b):
    return lax.dot_general(a, b, (((1,), (0,)), ((), ())), preferred_element_type=F32)


def split_terms(value, count):
    terms = []
    for _ in range(count):
        terms.append(value.astype(BF16).astype(F32))
        value = value - terms[-1]
    return terms


def prepare_body(reach_ref, q_in, s_in, v_in, g_in, k_ref, v_ref, g_ref, q_ref, s_ref, sems):
    length, width = q_ref.shape
    pairs = ((q_in, q_ref), (s_in, s_ref), (v_in, v_ref), (g_in, g_ref))
    copies = [pltpu.make_async_copy(a, b, sems.at[i]) for i, (a, b) in enumerate(pairs)]
    for copy in copies:
        copy.start()
    copies[0].wait()
    copies[1].wait()
    row = lax.broadcasted_iota(jnp.int32, (LANES, LANES), 0)
    lane = lax.broadcasted_iota(jnp.int32, (LANES, LANES), 1)
    same = jnp.where(lax.div(row, HD) == lax.div(lane, HD), 1.0, 0.0).astype(BF16)
    scale_terms = split_terms(s_ref[...], 3)
    scale_terms.append(jnp.zeros((LANES - 3 * s_ref.shape[0], length), F32))
    scale_terms = jnp.transpose(jnp.concatenate(scale_terms, axis=0)).astype(BF16)
    for g in range(width // LANES):
        lanes = slice(LANES * g, LANES * g + LANES)
        q = q_ref[:, lanes].astype(F32)
        high, rest = split_terms(q * q, 2)
        total = dot_nn(high.astype(BF16), same) + dot_nn(rest.astype(BF16), same)
        head = 2 * g + lax.div(lane, HD)
        pick = jnp.where(lax.rem(row, s_ref.shape[0]) == head, 1.0, 0.0)
        pick = jnp.where(row < 3 * s_ref.shape[0], pick, 0.0).astype(BF16)
        scale = dot_nn(scale_terms, pick)
        k_ref[g * length : g * length + length, :] = ((q * lax.rsqrt(total + 1e-6)) * scale).astype(BF16)
    reach = jnp.full((REACH_ROWS, LANES), reach_ref[0].astype(F32), F32)
    k_ref[width // LANES * length :, :] = reach.astype(BF16)
    copies[2].wait()
    copies[3].wait()


def turn_body(k_ref, v_ref, g_ref, vt_ref, gt_ref, pair_ref, minus_ref):
    length, width = v_ref.shape
    heads = width // HD
    vt_ref[...] = jnp.transpose(v_ref[...].astype(F32)).astype(BF16)
    gt_ref[...] = jnp.transpose(g_ref[...].astype(F32)).astype(BF16)
    lane = lax.broadcasted_iota(jnp.int32, (length, LANES), 1)
    for h in range(heads):
        rows = k_ref[h // 2 * length : h // 2 * length + length, :]
        keep = (lane < HD) if h % 2 == 0 else (lane >= HD)
        alone = jnp.where(keep, rows, jnp.zeros_like(rows))
        for part in range(0, length, LANES):
            at = h // 2 * 2 * length + 2 * part + h % 2 * LANES
            pair_ref[at : at + LANES, :] = alone[part : part + LANES, :]
        term = lane - ((HD if h % 2 == 0 else 0) + h)
        one = jnp.logical_or(term == 0, jnp.logical_or(term == heads, term == 2 * heads))
        minus = jnp.where(one, -1.0, 0.0).astype(BF16)
        minus_ref[h * length : h * length + length, :] = jnp.where(keep, rows, minus)


def join_body(*refs):
    *parts, out_ref = refs
    at = 0
    for ref in parts:
        out_ref[at : at + ref.shape[0], :] = ref[...]
        at += ref.shape[0]


NEAR = ((0, 0, 0, None), (1, 0, 1, None))
DIRECT = ((0, 0, 2, 1), (0, 1, 1, 1), (1, 0, 4, 2), (1, 1, 3, 2))
SIBLING = ((0, 0, 1, None),)
PASSED = ((0, 0, 3, -1), (0, 1, 2, -1), (1, 1, 4, -2))


def blocks(slots):
    return 1 if slots is NEAR or slots is SIBLING else 2


def allowed_slots(chips, reach_ref, slots, keys):
    place = lax.axis_index("seq")
    chip, toward = lax.div(place, 2), 2 * lax.rem(place, 2) - 1
    near = reach_ref[0].astype(F32)
    result = []
    for index, block, distance, away in slots:
        if distance == 0:
            result.append(None)
            continue
        start = (block + 1) * (keys[index].shape[0] // blocks(slots)) - REACH_ROWS
        far = jnp.max(keys[index][start : start + REACH_ROWS, 0:LANES].astype(F32))
        allowed = jnp.minimum(near, far) >= float(distance)
        if away is not None:
            other = chip + away * toward
            allowed = jnp.logical_and(allowed, jnp.logical_and(other >= 0, other < chips))
        result.append(allowed)
    return result


def off_diagonal(scores, row, column):
    rows = lax.broadcasted_iota(jnp.int32, scores.shape, 0) + row
    columns = lax.broadcasted_iota(jnp.int32, scores.shape, 1) + column
    return jnp.where(rows == columns, NEGATIVE, scores)


def stats_body(chips, slots, reach_ref, paired, *refs):
    *refs, ok_ref = refs
    count = len({slot[0] for slot in slots})
    keys, rest = refs[:count], refs[count:]
    last = slots is PASSED
    if last:
        near_ref, direct_ref, m_ref, w_ref, total_ref, f_ref, shift_ref = rest
    else:
        m_ref, w_ref = rest
    length = m_ref.shape[1]
    heads = paired.shape[0] // length

    def tile(index):
        array, block, distance, _ = slots[index]
        products = []
        for g in range(heads // 2):
            row = block * (heads // 2 * length + REACH_ROWS) + g * length
            rows = keys[array][row : row + length, :]
            for part in range(0, length, LANES):
                at = 2 * (g * length + part)
                products.append((g, part, dot_nt(rows, paired[at : at + 2 * LANES, :])))
        for g, part, product in products:
            for h in (2 * g, 2 * g + 1):
                scores = product[:, LANES * (h % 2) : LANES * (h % 2) + LANES]
                if distance == 0:
                    scores = off_diagonal(scores, 0, part)
                top = jnp.max(scores, axis=0, keepdims=True)
                exponent = jnp.exp(scores - top)
                total = jnp.sum(exponent, axis=0, keepdims=True)
                lanes = slice(part, part + LANES)
                at = 2 * heads * index + h
                m_ref[at : at + 1, lanes] = top
                m_ref[at + heads : at + heads + 1, lanes] = total
                at = (index * heads + h) * length * (length // LANES) + part // LANES * length
                w_ref[at : at + length, :] = exponent.astype(BF16)

    allowed = allowed_slots(chips, reach_ref, slots, keys)
    for index, ok in enumerate(allowed):
        if ok is None:
            ok_ref[index] = 1
            tile(index)
            continue
        ok_ref[index] = ok.astype(jnp.int32)
        at = 2 * heads * index
        m_ref[at : at + heads, :] = jnp.full((heads, length), NEGATIVE, F32)
        m_ref[at + heads : at + 2 * heads, :] = jnp.zeros((heads, length), F32)
        pl.when(ok)(partial(tile, index))

    if last:
        parts = []
        for ref, part in ((near_ref, NEAR), (direct_ref, DIRECT), (m_ref, PASSED)):
            parts += [(ref, 2 * heads * s) for s in range(len(part))]
        tops = [ref[at : at + heads, :] for ref, at in parts]
        top = tops[0]
        for other in tops[1:]:
            top = jnp.maximum(top, other)
        total = jnp.zeros((heads, length), F32)
        for index, (ref, at) in enumerate(parts):
            factor = jnp.exp(tops[index] - top)
            total = total + factor * ref[at + heads : at + 2 * heads, :]
            f_ref[2 * heads * index : 2 * heads * index + heads, :] = factor
        terms = split_terms(top + jnp.log(total), 3)
        terms.append(jnp.zeros((SHIFT_ROWS - 3 * heads, length), F32))
        shift_ref[...] = jnp.concatenate(terms, axis=0).astype(BF16)
        total_ref[...] = total


def numerator(values, w_ref, slots, index, h, length, heads):
    array, block, _, _ = slots[index]
    at = (index * heads + h) * length * (length // LANES)
    starts = range(at, at + length * (length // LANES), length)
    weights = [w_ref[start : start + length, :] for start in starts]
    row = (block * heads + h) * HD
    return dot_nn(values[array][row : row + HD, :], jnp.concatenate(weights, axis=1))


def attend_near_body(own, sib, w_ref, *outs):
    width, length = outs[0].shape
    heads = width // HD
    for index, out in enumerate(outs):
        for h in range(heads):
            part = numerator((own, sib), w_ref, NEAR, index, h, length, heads)
            out[HD * h : HD * h + HD, :] = part


def attend_body(slots, ok_ref, *refs):
    values, refs = refs[0:2], refs[2:]
    last = slots is PASSED
    if last:
        w_ref, f_ref, total_ref, acc_in, keep_ref, send_ref, acc, rows_ref = refs
    else:
        ok_sib, values, refs = values[0], (values[1], refs[0]), refs[1:]
        w_ref, f_ref, own_in, sib_in, acc = refs
    width, length = acc.shape
    heads = width // HD
    before = len(NEAR) + (len(DIRECT) if last else 0)

    def factor(slot, h):
        at = 2 * heads * slot + h
        return f_ref[at : at + 1, :]

    def tile(index):
        for h in range(heads):
            numer = numerator(values, w_ref, slots, index, h, length, heads)
            acc[HD * h : HD * h + HD, :] += numer * factor(before + index, h)

    def near():
        for h in range(heads):
            part = slice(HD * h, HD * h + HD)
            acc[part, :] += sib_in[part, :] * factor(1, h)

    if last:
        acc[...] = acc_in[...]
    else:
        for h in range(heads):
            part = slice(HD * h, HD * h + HD)
            acc[part, :] = own_in[part, :] * factor(0, h)
        pl.when(ok_sib[1] > 0)(near)
    for index in range(len(slots)):
        pl.when(ok_ref[index] > 0)(partial(tile, index))
    if last:
        for h in range(heads):
            part = slice(HD * h, HD * h + HD)
            acc[part, :] = acc[part, :] / total_ref[h : h + 1, :]
        rows_ref[...] = jnp.transpose(acc[...])
        half = length // 2
        mine = lax.axis_index("head")
        keep_ref[...] = rows_ref[pl.ds(pl.multiple_of(mine * half, half), half), :].astype(BF16)
        other = pl.multiple_of((1 - mine) * half, half)
        send_ref[...] = rows_ref[pl.ds(other, half), :].astype(BF16)


def shift_terms(ref, block, length):
    terms = ref[block * SHIFT_ROWS : (block + 1) * SHIFT_ROWS, :].astype(F32)
    rest = jnp.zeros((HD - SHIFT_ROWS, length), F32)
    return jnp.transpose(jnp.concatenate([terms, rest, terms, rest], axis=0)).astype(BF16)


def grad_tile(mine, key, grad, terms, block, length, width, heads, acc, own):
    low = lax.broadcasted_iota(jnp.int32, (length, LANES), 1) < HD
    row = block * (width // LANES * length + REACH_ROWS)
    products = []
    for h in heads:
        far = key[row + h // 2 * length : row + h // 2 * length + length, :]
        far = jnp.where(low if h % 2 == 0 else ~low, far, terms)
        products.append(dot_nt(far, mine[h * length : h * length + length, :]))
    if own:
        products = [off_diagonal(scores, 0, 0) for scores in products]
    weights = [jnp.exp(scores).astype(BF16) for scores in products]
    for h, weight in zip(heads, weights):
        part = slice(HD * h, HD * h + HD)
        share = dot_nn(grad[block * width + HD * h : block * width + HD * h + HD, :], weight)
        if own:
            acc[part, :] = share
        else:
            acc[part, :] += share


def grad_own_body(mine, key, grad, shift, acc):
    width, length = acc.shape
    heads = range(width // HD)
    terms = shift_terms(shift, 0, length)
    grad_tile(mine, key, grad, terms, 0, length, width, heads, acc, True)


def grad_body(slots, ok_ref, mine, *refs):
    count = len({slot[0] for slot in slots})
    keys, grads, shifts = refs[0:count], refs[count : 2 * count], refs[2 * count : 3 * count]
    acc_in, acc = refs[3 * count :]
    width, length = acc.shape
    heads = range(width // HD)
    acc[...] = acc_in[...]

    def tile(array, block):
        terms = shift_terms(shifts[array], block, length)
        key, grad = keys[array], grads[array]
        grad_tile(mine, key, grad, terms, block, length, width, heads, acc, False)

    for index, (array, block, _, _) in enumerate(slots):
        at = index + (len(NEAR) - 1 if slots is SIBLING else 0)
        pl.when(ok_ref[at] > 0)(partial(tile, array, block))


def final_body(ok_ref, keep_ref, got_ref, near_ref, far_ref, mine, acc_in, *refs):
    keys, grads, shifts, rest = refs[0:2], refs[2:4], refs[4:6], refs[6:]
    mixed_out, grad_out, acc, mixed, turned, sems = rest
    width, length = acc.shape
    total = dot_nn(keep_ref[...], near_ref[...]) + dot_nn(got_ref[...], far_ref[...])
    mixed[...] = total.astype(BF16)
    copies = [pltpu.make_async_copy(mixed, mixed_out, sems.at[0])]
    copies[0].start()
    acc[...] = acc_in[...]

    def tile(index):
        array, block, _, _ = PASSED[index]
        heads, terms = range(width // HD), shift_terms(shifts[array], block, length)
        key, grad = keys[array], grads[array]
        grad_tile(mine, key, grad, terms, block, length, width, heads, acc, False)

    for index in range(len(PASSED)):
        pl.when(ok_ref[index] > 0)(partial(tile, index))
    for group in range(width // LANES):
        lanes = slice(LANES * group, LANES * group + LANES)
        turned[group] = jnp.transpose(acc[lanes, :]).astype(BF16)
        copy = pltpu.make_async_copy(turned.at[group], grad_out.at[:, lanes], sems.at[group + 1])
        copy.start()
        copies.append(copy)
    for copy in copies:
        copy.wait()


VMEM = pl.BlockSpec(memory_space=pltpu.VMEM)
SMEM = pl.BlockSpec(memory_space=pltpu.SMEM)
HBM = pl.BlockSpec(memory_space=pltpu.HBM)
PARAMS = pltpu.CompilerParams(vmem_limit_bytes=8 * 1024 * 1024)


def call(body, scalars, args, outs, scratch=(), flags=0):
    args = [pltpu.with_memory_space_constraint(a, pltpu.VMEM) for a in args]
    run = pl.pallas_call(
        body,
        in_specs=[SMEM] * len(scalars) + [VMEM] * len(args),
        out_specs=[VMEM] * len(outs) + [SMEM] * (flags > 0),
        out_shape=[pltpu.VMEM(shape, dtype) for shape, dtype in outs]
        + [pltpu.SMEM((flags,), jnp.int32)] * (flags > 0),
        compiler_params=PARAMS,
        scratch_shapes=[pltpu.VMEM(shape, dtype) for shape, dtype in scratch],
    )
    return list(run(*scalars, *args))


def joined(parts):
    rows, width = sum(part.shape[0] for part in parts), parts[0].shape[1]
    (both,) = call(join_body, [], parts, [((rows, width), BF16)])
    return both


def gathered(own):
    sib = sibling(own)
    return [own, sib], *rings(joined([own, sib]))


def rings(both):
    one, two = chip_ring(both, 1), chip_ring(both, 2)
    one, two = lax.optimization_barrier((one, two))
    return [one, two], [sibling(one), sibling(two)]


def compute(queries, values, scales, block_reach, out_weight, out_grad):
    length, width = queries.shape
    heads = scales.shape[1]
    chips = lax.axis_size("seq") // 2
    inputs = [queries, scales.T, values, out_grad]
    keys, *raw = pl.pallas_call(
        prepare_body,
        name="prepare",
        in_specs=[SMEM] + [HBM] * 4,
        out_specs=[VMEM] * 3,
        out_shape=[
            pltpu.VMEM((width // LANES * length + REACH_ROWS, LANES), BF16),
            pltpu.VMEM((length, width), BF16),
            pltpu.VMEM((length, width), BF16),
        ],
        compiler_params=PARAMS,
        scratch_shapes=[
            pltpu.VMEM((length, width), BF16),
            pltpu.VMEM((heads, length), F32),
            pltpu.SemaphoreType.DMA((4,)),
        ],
    )(block_reach, *(pltpu.with_memory_space_constraint(a, pltpu.HBM) for a in inputs))
    outs = [((width, length), BF16)] * 2 + [((heads * length, LANES), BF16)] * 2
    turned, grads, paired, shifted = call(turn_body, [], [keys, *raw], outs)
    stages = (NEAR, DIRECT, PASSED)
    key_set = gathered(keys)
    value_set = gathered(turned)
    grad_set = gathered(grads)
    far_weight = other_head(out_weight)

    tops, weights, allowed = [], [], []
    for index, slots in enumerate(stages):
        last = slots is PASSED
        outs = [
            ((2 * heads * len(slots), length), F32),
            ((heads * len(slots) * length * length // LANES, LANES), BF16),
        ]
        if last:
            total = sum(len(part) for part in stages)
            outs += [((heads, length), F32), ((2 * heads * total, length), F32)]
            outs += [((SHIFT_ROWS, length), BF16)]
        args = [paired, *key_set[index], *(tops if last else [])]
        body = partial(stats_body, chips, slots)
        top, weight, *rest, ok = call(body, [block_reach], args, outs, flags=len(slots))
        tops.append(top)
        weights.append(weight)
        allowed.append(ok)
    totals, factors, shifts = rest
    shift_set = gathered(shifts)

    whole = ((width, length), F32)
    near = call(attend_near_body, [], [*value_set[0], weights[0]], [whole] * 2)
    args = [*value_set[1], weights[1], factors, *near]
    (running,) = call(
        lambda ok_sib, ok, *refs: attend_body(DIRECT, ok, ok_sib, *refs),
        [allowed[0], allowed[1]],
        args,
        [whole],
    )
    args = [*value_set[2], weights[2], factors, totals, running]
    outs = [((length // 2, width), BF16)] * 2
    scratch = [whole, ((length, width), F32)]
    body = partial(attend_body, PASSED)
    keep, send = call(body, [allowed[2]], args, outs, scratch)
    got = other_head(send)

    args = [shifted, keys, grads, shifts]
    running = call(grad_own_body, [], args, [whole])
    sets = (key_set, grad_set, shift_set)
    args = [shifted, *(part[0][1] for part in sets), *running]
    running = call(partial(grad_body, SIBLING), [allowed[0]], args, [whole])
    args = [shifted, *key_set[1], *grad_set[1], *shift_set[1], *running]
    (running,) = call(partial(grad_body, DIRECT), [allowed[1]], args, [whole])
    half, full = length // 2, out_weight.shape[1]
    inputs = [keep, got, out_weight, far_weight, shifted, running]
    inputs += [*key_set[2], *grad_set[2], *shift_set[2]]
    inputs = [pltpu.with_memory_space_constraint(a, pltpu.VMEM) for a in inputs]
    mixed, value_grad = pl.pallas_call(
        final_body,
        name="final",
        in_specs=[SMEM] + [VMEM] * len(inputs),
        out_specs=[HBM] * 2,
        out_shape=[
            jax.ShapeDtypeStruct((half, full), BF16),
            jax.ShapeDtypeStruct((length, width), BF16),
        ],
        compiler_params=PARAMS,
        scratch_shapes=[
            pltpu.VMEM((width, length), F32),
            pltpu.VMEM((half, full), BF16),
            pltpu.VMEM((width // LANES, length, LANES), BF16),
            pltpu.SemaphoreType.DMA((1 + width // LANES,)),
        ],
    )(allowed[2], *inputs)
    return (mixed, value_grad)


def solution(mesh):
    return jax.shard_map(
        compute,
        mesh=mesh,
        in_specs=(
            P("seq", "head"),
            P("seq", "head"),
            P("seq", "head"),
            P("seq"),
            P("head", None),
            P("seq", "head"),
        ),
        out_specs=(P(("seq", "head"), None), P("seq", "head")),
        check_vma=False,
    )
```
